256 devices in a mesh: ia: 8 (over z), ja: 32 (over y, x, core).
Axes of the slice: x: 4, y: 4, z: 8, core: 2. Of those that a mesh axis runs over, the one named last changes fastest.
Arguments:
- pno_basis: bfloat16 [8, 64, 512, 128], P('ia', 'ja'), may hold values from -0.4375 to 0.4375
- domain_map: int32 [8, 64, 512], replicated, may hold values from 0 to 1023, as said below
- amplitudes: float32 [8, 64, 128, 128], P('ia', 'ja'), may hold values from -6 to 6
- exchange_ints: float32 [8, 64, 128, 128], P('ia', 'ja'), may hold values from -6 to 6
- pno_energy: float32 [8, 64, 128], P('ia', 'ja'), may hold values from 0.5 to 3
- row_energy: float32 [8], P('ia'), may hold values from -1.5 to -0.3
- column_energy: float32 [64], P('ja'), may hold values from -1.5 to -0.3
- coupling_rows: float32 [8, 8], P('ia'), may hold values from -0.6 to 0.6
- coupling_columns: float32 [64, 64], P(None, 'ja'), may hold values from -0.6 to 0.6
- row_neighbours: int32 [8, 64, 6], P('ia', 'ja'), may hold values from 0 to 7, as said below
- column_neighbours: int32 [8, 64, 24], P('ia', 'ja'), may hold values from 0 to 63, as said below
- row_counts: int32 [8, 64], P('ia', 'ja'), may hold values from 1 to 6
- column_counts: int32 [8, 64], P('ia', 'ja'), may hold values from 1 to 24
Outputs:
- new_amplitudes: float32 [8, 64, 128, 128], P('ia', 'ja')
- pair_energy: float32 [8, 64], P('ia', 'ja')
The draws below stay inside these ranges and needn't reach their ends.
Inputs may be any that keep to these rules, and one draw needn't show every extreme that they name: `domain_map`: the 512 entries of one pair are distinct. `row_neighbours`: the 6 entries of a pair (i, j) are distinct and differ from i. `column_neighbours`: the 24 entries of a pair (i, j) are distinct and differ from j.
All inputs are finite; a program needn't handle non-finite values.
Results may differ from the reference program's by a relative error of at most 0.008.
Values may be sent and summed in bfloat16 or wider, within the bound.
No kernel may reach another device: no remote copies, remote signals or barrier semaphores. Data moves between devices by JAX's collectives and lax.ppermute only.
A program may use at most 64 MiB of HBM per device.

```python
import jax
import jax.numpy as jnp
from jax import lax

NP = 128
NDOM = 512
NVG = 1024
ITERS = 2
NI = 8
NJ = 64
KR = 6
KC = 24


def distinct_picks(key, groups, universe, picked):
    scores = jax.random.randint(key, (groups, universe), 0, 1 << 20) * universe + jnp.arange(universe, dtype=jnp.int32)[None, :]
    return jnp.argsort(scores, axis=1, stable=True)[:, :picked].astype(jnp.int32)


def draw_domain_map(key, part):
    chosen = distinct_picks(jax.random.fold_in(key, 11), NI * NJ, NVG, NDOM)
    return chosen.reshape(NI, NJ, NDOM)


def draw_row_neighbours(key, part):
    chosen = distinct_picks(jax.random.fold_in(key, 12), NI * NJ, NI - 1, KR).reshape(NI, NJ, KR)
    own_rows = jnp.arange(NI, dtype=jnp.int32)[:, None, None]
    return jnp.where(chosen >= own_rows, chosen + 1, chosen)


def draw_column_neighbours(key, part):
    chosen = distinct_picks(jax.random.fold_in(key, 13), NI * NJ, NJ - 1, KC).reshape(NI, NJ, KC)
    own_columns = jnp.arange(NJ, dtype=jnp.int32)[None, :, None]
    return jnp.where(chosen >= own_columns, chosen + 1, chosen)


def plant(values, stream_key, least, top_value):
    longest = values.shape.index(max(values.shape))
    spots = []
    for shift in (0, 1):
        where = [jax.random.randint(jax.random.fold_in(stream_key, axis), (), 0, length) for axis, length in enumerate(values.shape)]
        where[longest] = (where[longest] + shift) % values.shape[longest]
        spots.append(tuple(where))
    return values.at[spots[0]].set(least).at[spots[1]].set(top_value)


def shard_levels(rng, shape, split, least, top_value):
    level = 1.0
    for position, shards_of in split:
        draws = jax.random.uniform(jax.random.fold_in(jax.random.fold_in(rng, 6), position), (shards_of,), jnp.float32, least / len(split), top_value / len(split))
        level = level * jnp.repeat(jnp.exp(draws), shape[position] // shards_of).reshape((-1,) + (1,) * (len(shape) - 1 - position))
    return level


def noise(key, shape, width, limit, pieces=(), held_as=jnp.bfloat16):
    loudness = shard_levels(key, shape, pieces, -0.22, 0.18) if pieces else 1.0
    entries = jax.random.normal(key, shape, jnp.float32) * width * loudness
    return jnp.minimum(jnp.maximum(entries, -limit), limit).astype(held_as)


def setup_inputs(seed: int = 0) -> dict:
    streams_of = jax.random.split(jax.random.key(seed), 14)
    return {
        "pno_basis": noise(streams_of[0], (NI, NJ, NDOM, NP), (NDOM * 35 // 100) ** -0.5, 0.4375, ((0, 8), (1, 32))),
        "domain_map": draw_domain_map(jax.random.fold_in(streams_of[13], 71), 0),
        "amplitudes": noise(streams_of[2], (NI, NJ, NP, NP), 1.0, 6.0, ((0, 8), (1, 32)), jnp.float32),
        "exchange_ints": noise(streams_of[3], (NI, NJ, NP, NP), 1.0, 6.0, ((0, 8), (1, 32)), jnp.float32),
        "pno_energy": jnp.clip(0.5 + 2.5 * jax.random.uniform(streams_of[4], (NI, NJ, NP), jnp.float32) ** shard_levels(streams_of[4], (NI, NJ, NP), ((0, 8), (1, 32)), -0.2, 0.2), 0.5, 3.0),
        "row_energy": jnp.clip(-1.5 + 1.2 * jax.random.uniform(streams_of[5], (NI,), jnp.float32) ** shard_levels(streams_of[5], (NI,), ((0, 8),), -0.2, 0.2), -1.5, -0.3),
        "column_energy": jnp.clip(-1.5 + 1.2 * jax.random.uniform(streams_of[6], (NJ,), jnp.float32) ** shard_levels(streams_of[6], (NJ,), ((0, 32),), -0.2, 0.2), -1.5, -0.3),
        "coupling_rows": jnp.clip(jax.random.uniform(streams_of[7], (NI, NI), jnp.float32, -0.6, 0.6) * shard_levels(streams_of[7], (NI, NI), ((0, 8),), -0.4, 0.0), -0.6, 0.6),
        "coupling_columns": jnp.clip(jax.random.uniform(streams_of[8], (NJ, NJ), jnp.float32, -0.6, 0.6) * shard_levels(streams_of[8], (NJ, NJ), ((1, 32),), -0.4, 0.0), -0.6, 0.6),
        "row_neighbours": draw_row_neighbours(jax.random.fold_in(streams_of[13], 71), 0),
        "column_neighbours": draw_column_neighbours(jax.random.fold_in(streams_of[13], 71), 0),
        "row_counts": plant(jax.random.randint(streams_of[11], (NI, NJ), 1, KR + 1), jax.random.fold_in(streams_of[11], 1), 1, KR).astype(jnp.int32),
        "column_counts": plant(jax.random.randint(streams_of[12], (NI, NJ), 1, KC + 1), jax.random.fold_in(streams_of[12], 1), 1, KC).astype(jnp.int32),
    }


level_shift = 0.3


def embed_basis(domain_entries, basis_block):
    zeroed = jnp.zeros((NVG, basis_block.shape[1]), basis_block.dtype)
    return zeroed.at[domain_entries].set(basis_block)


def reference(pno_basis, domain_map, amplitudes, exchange_ints, pno_energy, row_energy, column_energy, coupling_rows, coupling_columns, row_neighbours, column_neighbours, row_counts, column_counts):
    pair_count = NI * NJ
    flat_basis = pno_basis.reshape(pair_count, NDOM, NP)
    flat_domain = domain_map.reshape(pair_count, NDOM)
    embedded = jax.vmap(embed_basis)(flat_domain, flat_basis)
    row_ids = jnp.arange(NI, dtype=jnp.int32)[:, None, None]
    column_ids = jnp.arange(NJ, dtype=jnp.int32)[None, :, None]
    row_partner = (row_neighbours * NJ + column_ids).reshape(pair_count, KR)
    column_partner = (row_ids * NJ + column_neighbours).reshape(pair_count, KC)
    row_live = jnp.arange(KR, dtype=jnp.int32)[None, None, :] < row_counts[:, :, None]
    column_live = jnp.arange(KC, dtype=jnp.int32)[None, None, :] < column_counts[:, :, None]
    row_weight = jnp.where(row_live, coupling_rows[row_ids, row_neighbours], 0.0).reshape(pair_count, KR)
    column_weight = jnp.where(column_live, coupling_columns[column_neighbours, column_ids], 0.0).reshape(pair_count, KC)
    energy_gap = pno_energy[:, :, :, None] + pno_energy[:, :, None, :] - row_energy[:, None, None, None] - column_energy[None, :, None, None]
    current = amplitudes
    for iteration in range(ITERS):
        rounded = current.astype(jnp.bfloat16).reshape(pair_count, NP, NP)

        def couple_pair(pair_index):
            own_basis = flat_basis[pair_index].astype(jnp.float32)
            own_domain = flat_domain[pair_index]

            def neighbour_term(partner, weight):
                matched = embedded[partner][own_domain].astype(jnp.float32)
                intersection = jnp.dot(own_basis.T, matched).astype(jnp.bfloat16)
                intersection_wide = intersection.astype(jnp.float32)
                halved = jnp.dot(intersection_wide, rounded[partner].astype(jnp.float32)).astype(jnp.bfloat16)
                return weight * jnp.dot(halved.astype(jnp.float32), intersection_wide.T)

            from_rows = jnp.sum(jax.vmap(neighbour_term)(row_partner[pair_index], row_weight[pair_index]), axis=0)
            from_columns = jnp.sum(jax.vmap(neighbour_term)(column_partner[pair_index], column_weight[pair_index]), axis=0)
            return from_rows + from_columns

        coupled = lax.map(couple_pair, jnp.arange(pair_count, dtype=jnp.int32)).reshape(NI, NJ, NP, NP)
        residual = exchange_ints + energy_gap * current - coupled
        current = current - residual / (energy_gap + level_shift)
    pair_energy = jnp.sum(exchange_ints * (2.0 * current - jnp.swapaxes(current, 2, 3)), axis=(2, 3))
    return current, pair_energy
```

```python
import functools

import jax
import jax.numpy as jnp
from jax import lax
from jax.experimental import pallas as pl
from jax.experimental.pallas import tpu as pltpu
from jax.sharding import PartitionSpec as P

ITERS = 2
level_shift = 0.3

NX = 4
NY = 4
CORES = 2
ROWS = NX * NY * CORES
RING = 8
PAIRS = 2
KR = 6
KC = 24
CHUNKS = 5
ZCHUNK = 4
LIST = 34


VMEM = pltpu.MemorySpace.VMEM
SMEM = pltpu.MemorySpace.SMEM


def ring_perm(step):
    return [(z, (z + step) % RING) for z in range(RING)]


def mixed_perm(step, first):
    moves = []
    for y in range(NY):
        for x in range(NX):
            for c in range(CORES):
                if (c == 0) == first:
                    ty, tx = y, (x + step) % NX
                else:
                    ty, tx = (y + step) % NY, x
                moves.append(((y * NX + x) * CORES + c, (ty * NX + tx) * CORES + c))
    return moves


def core_perm():
    return [(d, d ^ 1) for d in range(ROWS)]


def swap(x):
    return lax.ppermute(x, "ja", core_perm())


def stage(x, step, first):
    return lax.ppermute(x, "ja", mixed_perm(step, first))


def plan_body(where, rown, coln, rowc, colc, crow, ccol, items, weights, counts):
    z = where[0]
    here = where[1]
    y = here // (NX * CORES)
    x = (here // CORES) % NX
    c = here % CORES
    for n in range(CHUNKS):
        counts[n] = 0

    def put(chunk, p, pos, dom, w):
        at = chunk * LIST + counts[chunk]
        items[at * 3] = p
        items[at * 3 + 1] = pos
        items[at * 3 + 2] = dom
        weights[at] = w
        counts[chunk] = counts[chunk] + 1

    for p in range(PAIRS):

        def row_slot(s, _):
            k = rown[p, s]
            rel = (k - z + RING) % RING
            put(ZCHUNK, p, (rel - 1) * PAIRS + p, ROWS * PAIRS + k * PAIRS + p, crow[0, k])
            return 0

        lax.fori_loop(0, rowc[0, p], row_slot, 0)

        def column_slot(s, _):
            k = coln[p, s]
            there = k // PAIRS
            rx = (there // CORES) % NX - x
            ry = there // (NX * CORES) - y
            rx = (rx + NX) % NX
            ry = (ry + NY) % NY
            tc = there % CORES
            m = jnp.where(tc == 0, rx, ry)
            n = jnp.where(tc == 0, ry, rx)
            other = jnp.where(tc == c, 0, 1)
            put(n, p, (other * NX + m) * PAIRS + k % PAIRS, k, ccol[k, p])
            return 0

        lax.fori_loop(0, colc[0, p], column_slot, 0)

    for n in range(CHUNKS):
        at = n * LIST + counts[n]
        for extra in range(2):
            items[(at + extra) * 3] = 0
            items[(at + extra) * 3 + 1] = 0
            items[(at + extra) * 3 + 2] = 0
            weights[at + extra] = 0.0


def make_plan(where, rown, coln, rowc, colc, crow, ccol):
    smem = pl.BlockSpec(memory_space=SMEM)
    return pl.pallas_call(
        plan_body,
        out_shape=(
            jax.ShapeDtypeStruct((CHUNKS * LIST * 3,), jnp.int32),
            jax.ShapeDtypeStruct((CHUNKS * LIST,), jnp.float32),
            jax.ShapeDtypeStruct((8,), jnp.int32),
        ),
        in_specs=[smem] * 7,
        out_specs=(smem, smem, smem),
        name="plan",
    )(where, rown, coln, rowc, colc, crow, ccol)


def nt(a, b):
    return lax.dot_general(a, b, (((1,), (1,)), ((), ())), preferred_element_type=jnp.float32)


def update(acc, exch, gap, cur):
    residual = exch + gap * cur - acc
    return cur - residual / (gap + level_shift)


def load_parts(parts, buf, sems):
    copies = []
    at = 0
    for index, part in enumerate(parts):
        size = part.shape[0]
        copies.append(pltpu.make_async_copy(part, buf.at[pl.ds(at, size)], sems.at[index]))
        at += size
    for copy in copies:
        copy.start()
    return copies


def first_body(chunk, nparts, width, depth, last, *refs):
    items, weights, counts, own_t, own_dom, doms, acc_in = refs[:7]
    refs = refs[7:]
    if last:
        exch, gap, cur = refs[:3]
        refs = refs[3:]
    parts, refs = refs[:nparts], refs[nparts:]
    if last:
        kept, out, rounded = refs[:3]
        acc, buf, domb, sems = refs[3:]
    else:
        kept, acc = refs[:2]
        buf, domb, sems = refs[2:]
    copies = load_parts(parts, buf, sems)
    acc[...] = acc_in[...]
    for p in range(PAIRS):
        domb[p] = jnp.broadcast_to(own_dom[p], (depth, width))
    for copy in copies:
        copy.wait()

    def one(item):
        at = chunk * LIST + item
        p = items[at * 3]
        pos = items[at * 3 + 1]
        dom = doms[pl.ds(items[at * 3 + 2], 1), :]
        w = weights[at]
        mine = domb[p]
        match = jnp.concatenate(
            [
                jnp.where(mine == dom[:, g * width : (g + 1) * width], 1.0, 0.0).astype(jnp.bfloat16)
                for g in range(depth // width)
            ],
            axis=1,
        )
        picked = jnp.dot(own_t[p], match, preferred_element_type=jnp.float32).astype(jnp.bfloat16)
        inter = jnp.dot(
            picked, buf[pos, :depth, :], preferred_element_type=jnp.float32
        ).astype(jnp.bfloat16)
        kept[item] = inter
        halved = jnp.dot(
            inter, buf[pos, depth:, :], preferred_element_type=jnp.float32
        ).astype(jnp.bfloat16)
        return p, w * nt(halved, inter)

    def two(step, _):
        pa, a = one(step * 2)
        pb, b = one(step * 2 + 1)
        acc[pa] += a
        acc[pb] += b
        return 0

    lax.fori_loop(0, (counts[chunk] + 1) // 2, two, 0)
    if last:
        for p in range(PAIRS):
            new = update(acc[p], exch[p], gap[p], cur[p])
            out[p] = new
            rounded[p] = new.astype(jnp.bfloat16)


def first_pass(chunk, plan, own_t, own_dom, doms, acc, parts, finish=None):
    vmem = pl.BlockSpec(memory_space=VMEM)
    smem = pl.BlockSpec(memory_space=SMEM)
    hbm = pl.BlockSpec(memory_space=pl.ANY)
    width = own_t.shape[1]
    depth = own_t.shape[2]
    total = sum(part.shape[0] for part in parts)
    last = finish is not None
    extra = list(finish) if last else []
    kept = jax.ShapeDtypeStruct((LIST, width, width), jnp.bfloat16)
    square = jax.ShapeDtypeStruct((PAIRS, width, width), jnp.float32)
    rounded = jax.ShapeDtypeStruct((PAIRS, width, width), jnp.bfloat16)
    scratch = [
        pltpu.VMEM((total, depth + width, width), jnp.bfloat16),
        pltpu.VMEM((PAIRS, depth, width), jnp.int32),
        pltpu.SemaphoreType.DMA((len(parts),)),
    ]
    if last:
        scratch = [pltpu.VMEM((PAIRS, width, width), jnp.float32)] + scratch
    out_shape = (kept, square, rounded) if last else (kept, square)
    return pl.pallas_call(
        functools.partial(first_body, chunk, len(parts), width, depth, last),
        out_shape=out_shape,
        in_specs=[smem] * 3 + [vmem] * (4 + len(extra)) + [hbm] * len(parts),
        out_specs=(vmem,) * len(out_shape),
        scratch_shapes=scratch,
        name="first%d" % chunk,
    )(*plan, own_t, own_dom, doms, acc, *extra, *parts)


def second_body(chunk, nparts, last, *refs):
    items, weights, counts, kept, acc_in = refs[:5]
    refs = refs[5:]
    if last:
        exch, gap, cur = refs[:3]
        refs = refs[3:]
    parts, refs = refs[:nparts], refs[nparts:]
    if last:
        out, energy, acc, buf, sems = refs
    else:
        acc, buf, sems = refs
    copies = load_parts(parts, buf, sems)
    acc[...] = acc_in[...]
    for copy in copies:
        copy.wait()

    def one(item):
        at = chunk * LIST + item
        p = items[at * 3]
        pos = items[at * 3 + 1]
        inter = kept[item]
        halved = jnp.dot(inter, buf[pos], preferred_element_type=jnp.float32).astype(jnp.bfloat16)
        return p, weights[at] * nt(halved, inter)

    def two(step, _):
        pa, a = one(step * 2)
        pb, b = one(step * 2 + 1)
        acc[pa] += a
        acc[pb] += b
        return 0

    lax.fori_loop(0, (counts[chunk] + 1) // 2, two, 0)
    if last:
        for p in range(PAIRS):
            new = update(acc[p], exch[p], gap[p], cur[p])
            out[p] = new
            terms = exch[p] * (2.0 * new - new.T)
            energy[p] = jnp.broadcast_to(jnp.sum(terms), energy.shape[1:])


def second_pass(chunk, plan, kept, acc, parts, finish=None):
    vmem = pl.BlockSpec(memory_space=VMEM)
    smem = pl.BlockSpec(memory_space=SMEM)
    hbm = pl.BlockSpec(memory_space=pl.ANY)
    width = kept.shape[1]
    total = sum(part.shape[0] for part in parts)
    last = finish is not None
    extra = list(finish) if last else []
    square = jax.ShapeDtypeStruct((PAIRS, width, width), jnp.float32)
    scratch = [
        pltpu.VMEM((total, width, width), jnp.bfloat16),
        pltpu.SemaphoreType.DMA((len(parts),)),
    ]
    if last:
        scratch = [pltpu.VMEM((PAIRS, width, width), jnp.float32)] + scratch
        out_shape = (square, jax.ShapeDtypeStruct((PAIRS, 8, width), jnp.float32))
        out_specs = (vmem, vmem)
    else:
        out_shape = square
        out_specs = vmem
    return pl.pallas_call(
        functools.partial(second_body, chunk, len(parts), last),
        out_shape=out_shape,
        in_specs=[smem] * 3 + [vmem] * (2 + len(extra)) + [hbm] * len(parts),
        out_specs=out_specs,
        scratch_shapes=scratch,
        name="second%d" % chunk,
    )(*plan, kept, acc, *extra, *parts)


def spread(block):
    near = {k: stage(block, k, True) for k in (1, 3, 2)}
    forward, backward = [], []
    f, b = block, block
    for step in range(4):
        f = lax.ppermute(f, "ia", ring_perm(1))
        forward.append(f)
        if step < 3:
            b = lax.ppermute(b, "ia", ring_perm(-1))
            backward.append(b)
    mine = jnp.concatenate([block, near[3], near[2], near[1]], axis=0)
    half = mine.shape[0] // 2
    from_low = stage(mine, 1, False)
    from_high = stage(mine, 3, False)
    far_low = stage(from_low[:half], 1, False)
    far_high = stage(from_high[half:], 3, False)
    return [
        [mine, swap(mine)],
        [from_high, swap(from_high)],
        [far_low, far_high, swap(far_low), swap(far_high)],
        [from_low, swap(from_low)],
        backward + forward[::-1],
    ]


ORDER = (0, 4, 3, 1, 2)


def local(
    pno_basis,
    domain_map,
    amplitudes,
    exchange_ints,
    pno_energy,
    row_energy,
    column_energy,
    coupling_rows,
    coupling_columns,
    row_neighbours,
    column_neighbours,
    row_counts,
    column_counts,
):
    z = lax.axis_index("ia")
    here = lax.axis_index("ja")
    width = amplitudes.shape[-1]
    basis = pno_basis[0]
    depth = basis.shape[1]
    block = jnp.concatenate([basis, amplitudes[0].astype(jnp.bfloat16)], axis=1)
    chunks = spread(block)
    where = jnp.stack([z, here]).astype(jnp.int32)
    plan = make_plan(
        where,
        row_neighbours[0],
        column_neighbours[0],
        row_counts,
        column_counts,
        coupling_rows,
        coupling_columns,
    )
    domain_rows = lax.dynamic_slice_in_dim(domain_map, z, 1, 0)[0]
    domain_columns = lax.dynamic_slice_in_dim(domain_map, here * PAIRS, PAIRS, 1)
    doms = jnp.concatenate([domain_rows, domain_columns.reshape(-1, depth)], axis=0)
    own_dom = lax.dynamic_slice_in_dim(domain_rows, here * PAIRS, PAIRS, 0)[:, :, None]
    own_t = jnp.swapaxes(basis, 1, 2)
    gap = (
        pno_energy[0, :, :, None]
        + pno_energy[0, :, None, :]
        - row_energy[0]
        - column_energy[:, None, None]
    )
    exch = exchange_ints[0]
    current = amplitudes[0]
    acc = jnp.zeros((PAIRS, width, width), jnp.float32)
    kept = {}
    for n in ORDER:
        if n == ORDER[-1]:
            kept[n], current, rounded = first_pass(
                n, plan, own_t, own_dom, doms, acc, chunks[n], (exch, gap, current)
            )
        else:
            kept[n], acc = first_pass(n, plan, own_t, own_dom, doms, acc, chunks[n])
    chunks = spread(rounded)
    acc = jnp.zeros((PAIRS, width, width), jnp.float32)
    for n in ORDER:
        if n == ORDER[-1]:
            current, energy = second_pass(n, plan, kept[n], acc, chunks[n], (exch, gap, current))
        else:
            acc = second_pass(n, plan, kept[n], acc, chunks[n])
    return current[None], energy[None, :, 0, 0]


def solution(mesh):
    in_specs = (
        P("ia", "ja", None, None),
        P(),
        P("ia", "ja", None, None),
        P("ia", "ja", None, None),
        P("ia", "ja", None),
        P("ia"),
        P("ja"),
        P("ia", None),
        P(None, "ja"),
        P("ia", "ja", None),
        P("ia", "ja", None),
        P("ia", "ja"),
        P("ia", "ja"),
    )
    out_specs = (P("ia", "ja", None, None), P("ia", "ja"))
    return jax.shard_map(local, mesh=mesh, in_specs=in_specs, out_specs=out_specs, check_vma=False)
```

```python
import functools

import jax
import jax.numpy as jnp
from jax import lax
from jax.experimental import pallas as pl
from jax.experimental.pallas import tpu as pltpu
from jax.sharding import PartitionSpec as P

level_shift = 0.3

NX = 4
NY = 4
CORES = 2
ROWS = NX * NY * CORES
RING = 8
PAIRS = 2
CHIP = PAIRS * CORES
CHUNKS = 5
ZCHUNK = 4
BATCH = 4
LIST = 36
GRANT = 16 * 1024 * 1024


VMEM = pltpu.MemorySpace.VMEM
SMEM = pltpu.MemorySpace.SMEM


def ring_perm(step):
    return [(z, (z + step) % RING) for z in range(RING)]


def mixed_perm(step, first):
    moves = []
    for y in range(NY):
        for x in range(NX):
            for c in range(CORES):
                if (c == 0) == first:
                    ty, tx = y, (x + step) % NX
                else:
                    ty, tx = (y + step) % NY, x
                moves.append(((y * NX + x) * CORES + c, (ty * NX + tx) * CORES + c))
    return moves


def core_perm():
    return [(d, d ^ 1) for d in range(ROWS)]


def swap(x):
    return lax.ppermute(x, "ja", core_perm())


def stage(x, step, first):
    return lax.ppermute(x, "ja", mixed_perm(step, first))


def plan_body(where, rown, coln, rowc, colc, crow, ccol, items, weights, counts):
    z = where[0]
    here = where[1]
    y = here // (NX * CORES)
    x = (here // CORES) % NX
    c = here % CORES
    for n in range(CHUNKS):
        counts[n] = 0

    def put(chunk, p, pos, dom, w):
        at = chunk * LIST + counts[chunk]
        items[at * 3] = p
        items[at * 3 + 1] = pos
        items[at * 3 + 2] = dom
        weights[at] = w
        counts[chunk] = counts[chunk] + 1

    for p in range(PAIRS):

        def row_slot(s, _):
            k = rown[p, s]
            rel = (k - z + RING) % RING
            put(ZCHUNK, p, (rel - 1) * PAIRS + p, ROWS * PAIRS + k * PAIRS + p, crow[0, k])
            return 0

        lax.fori_loop(0, rowc[0, p], row_slot, 0)

    for p in range(CHIP):

        def column_slot(s, _):
            k = coln[p, s]
            there = k // PAIRS

            @pl.when(there % CORES == c)
            def _():
                rx = ((there // CORES) % NX - x + NX) % NX
                ry = (there // (NX * CORES) - y + NY) % NY
                m = jnp.where(c == 0, rx, ry)
                n = jnp.where(c == 0, ry, rx)
                put(n, p, m * PAIRS + k % PAIRS, k, ccol[p, k])

            return 0

        lax.fori_loop(0, colc[p], column_slot, 0)

    for n in range(CHUNKS):
        at = n * LIST + counts[n]
        for extra in range(BATCH - 1):
            items[(at + extra) * 3] = 0
            items[(at + extra) * 3 + 1] = 0
            items[(at + extra) * 3 + 2] = 0
            weights[at + extra] = 0.0


def make_plan(where, rown, coln, rowc, colc, crow, ccol):
    smem = pl.BlockSpec(memory_space=SMEM)
    return pl.pallas_call(
        plan_body,
        out_shape=(
            jax.ShapeDtypeStruct((CHUNKS * LIST * 3,), jnp.int32),
            jax.ShapeDtypeStruct((CHUNKS * LIST,), jnp.float32),
            jax.ShapeDtypeStruct((8,), jnp.int32),
        ),
        in_specs=[smem] * 7,
        out_specs=(smem, smem, smem),
        compiler_params=pltpu.CompilerParams(vmem_limit_bytes=GRANT),
        cost_estimate=pl.CostEstimate(flops=0, transcendentals=0, bytes_accessed=6000000),
        name="plan",
    )(where, rown, coln, rowc, colc, crow, ccol)


def nt(a, b):
    return lax.dot_general(a, b, (((1,), (1,)), ((), ())), preferred_element_type=jnp.float32)


def load_parts(parts, buf, sems):
    copies = []
    at = 0
    for index, part in enumerate(parts):
        size = part.shape[0]
        copies.append(pltpu.make_async_copy(part, buf.at[pl.ds(at, size)], sems.at[index]))
        at += size
    for copy in copies:
        copy.start()
    return copies


def couple(chunk, items, weights, counts, kept, acc, amplitudes_of):
    def several(step, _):
        found = []
        for extra in range(BATCH):
            item = step * BATCH + extra
            at = chunk * LIST + item
            inter = kept[item]
            halved = jnp.dot(
                inter, amplitudes_of(items[at * 3 + 1]), preferred_element_type=jnp.float32
            ).astype(jnp.bfloat16)
            found.append((items[at * 3], weights[at] * nt(halved, inter)))
        for p, term in found:
            acc[p] += term
        return 0

    lax.fori_loop(0, (counts[chunk] + BATCH - 1) // BATCH, several, 0)


def first_body(chunk, nparts, width, depth, *refs):
    items, weights, counts, own_t, doms, acc_in = refs[:6]
    parts = refs[6 : 6 + nparts]
    kept, acc, domb = refs[6 + nparts : 9 + nparts]
    copies = []
    if nparts > 1:
        buf, sems = refs[9 + nparts :]
        copies = load_parts(parts, buf, sems)
    else:
        buf = parts[0]
    acc[...] = acc_in[...]
    columns = doms[doms.shape[0] - 8 :, :].T
    for p in range(CHIP):
        domb[p] = jnp.broadcast_to(columns[:, p : p + 1], (depth, width))
    for copy in copies:
        copy.wait()

    def several(step, _):
        for extra in range(BATCH):
            item = step * BATCH + extra
            at = chunk * LIST + item
            p = items[at * 3]
            pos = items[at * 3 + 1]
            dom = doms[pl.ds(items[at * 3 + 2], 1), :]
            mine = domb[p]
            match = jnp.concatenate(
                [
                    jnp.where(mine == dom[:, g * width : (g + 1) * width], 1.0, 0.0).astype(
                        jnp.bfloat16
                    )
                    for g in range(depth // width)
                ],
                axis=1,
            )
            picked = jnp.dot(own_t[p], match, preferred_element_type=jnp.float32)
            kept[item] = jnp.dot(
                picked.astype(jnp.bfloat16), buf[pos, :depth, :], preferred_element_type=jnp.float32
            ).astype(jnp.bfloat16)
        return 0

    lax.fori_loop(0, (counts[chunk] + BATCH - 1) // BATCH, several, 0)
    couple(chunk, items, weights, counts, kept, acc, lambda pos: buf[pos, depth:, :])


def first_pass(chunk, plan, own_t, doms, acc, parts):
    vmem = pl.BlockSpec(memory_space=VMEM)
    smem = pl.BlockSpec(memory_space=SMEM)
    hbm = pl.BlockSpec(memory_space=pl.ANY)
    width = own_t.shape[1]
    depth = own_t.shape[2]
    total = sum(part.shape[0] for part in parts)
    scratch = [pltpu.VMEM((CHIP, depth, width), jnp.int32)]
    if len(parts) > 1:
        scratch += [
            pltpu.VMEM((total, depth + width, width), jnp.bfloat16),
            pltpu.SemaphoreType.DMA((len(parts),)),
        ]
    return pl.pallas_call(
        functools.partial(first_body, chunk, len(parts), width, depth),
        out_shape=(
            jax.ShapeDtypeStruct((LIST, width, width), jnp.bfloat16),
            jax.ShapeDtypeStruct(acc.shape, jnp.float32),
        ),
        in_specs=[smem] * 3 + [vmem] * 3 + [hbm if len(parts) > 1 else vmem] * len(parts),
        out_specs=(vmem, vmem),
        scratch_shapes=scratch,
        compiler_params=pltpu.CompilerParams(vmem_limit_bytes=GRANT),
        cost_estimate=pl.CostEstimate(flops=0, transcendentals=0, bytes_accessed=10000000),
    )(*plan, own_t, doms, acc, *parts)


def second_body(chunk, nparts, *refs):
    items, weights, counts, kept, acc_in = refs[:5]
    parts = refs[5 : 5 + nparts]
    acc = refs[5 + nparts]
    copies = []
    if nparts > 1:
        buf, sems = refs[6 + nparts :]
        copies = load_parts(parts, buf, sems)
    else:
        buf = parts[0]
    acc[...] = acc_in[...]
    for copy in copies:
        copy.wait()
    couple(chunk, items, weights, counts, kept, acc, lambda pos: buf[pos])


def second_pass(chunk, plan, kept, acc, parts):
    vmem = pl.BlockSpec(memory_space=VMEM)
    smem = pl.BlockSpec(memory_space=SMEM)
    hbm = pl.BlockSpec(memory_space=pl.ANY)
    width = kept.shape[1]
    total = sum(part.shape[0] for part in parts)
    scratch = []
    if len(parts) > 1:
        scratch += [
            pltpu.VMEM((total, width, width), jnp.bfloat16),
            pltpu.SemaphoreType.DMA((len(parts),)),
        ]
    return pl.pallas_call(
        functools.partial(second_body, chunk, len(parts)),
        out_shape=jax.ShapeDtypeStruct(acc.shape, jnp.float32),
        in_specs=[smem] * 3 + [vmem] * 2 + [hbm if len(parts) > 1 else vmem] * len(parts),
        out_specs=vmem,
        scratch_shapes=scratch,
        compiler_params=pltpu.CompilerParams(vmem_limit_bytes=GRANT),
        cost_estimate=pl.CostEstimate(flops=0, transcendentals=0, bytes_accessed=3000000),
    )(*plan, kept, acc, *parts)


def final_body(exch, gap, cur, ours, theirs, out, energy):
    for p in range(PAIRS):
        residual = exch[p] + gap[p] * cur[p] - (ours[p] + theirs[p])
        new = cur[p] - residual / (gap[p] + level_shift)
        out[p] = new
        terms = exch[p] * (2.0 * new - new.T)
        energy[p] = jnp.broadcast_to(jnp.sum(terms), energy.shape[1:])


def final(exch, gap, cur, ours, theirs):
    width = exch.shape[1]
    vmem = pl.BlockSpec(memory_space=VMEM)
    return pl.pallas_call(
        final_body,
        out_shape=(
            jax.ShapeDtypeStruct((PAIRS, width, width), jnp.float32),
            jax.ShapeDtypeStruct((PAIRS, 8, width), jnp.float32),
        ),
        in_specs=[vmem] * 5,
        out_specs=(vmem, vmem),
        compiler_params=pltpu.CompilerParams(vmem_limit_bytes=GRANT),
        name="final",
    )(exch, gap, cur, ours, theirs)


def spread(block):
    def near(x, step):
        return stage(x, step, True)

    def far(x, step):
        return stage(x, step, False)

    def ring(x, step):
        return lax.ppermute(x, "ia", ring_perm(step))

    low = near(block, 1)
    high = near(block, 3)
    forward, backward = [], []
    f, b = block, block
    for step in range(4):
        f = ring(f, 1)
        forward.append(f)
        if step < 3:
            b = ring(b, -1)
            backward.append(b)
    middle = [near(low[:1], 1), near(high[1:], 3)]
    mine = jnp.concatenate([block, high, *middle, low], axis=0)
    half = mine.shape[0] // 2
    from_low = far(mine, 1)
    from_high = far(mine, 3)
    far_low = far(from_low[:half], 1)
    far_high = far(from_high[half:], 3)
    return [
        [mine],
        [from_high],
        [far_low, far_high],
        [from_low],
        backward + forward[::-1],
    ]


COLUMN_ORDER = (0, 3, 1, 2)


def whole(
    pno_basis,
    domain_map,
    amplitudes,
    exchange_ints,
    pno_energy,
    row_energy,
    column_energy,
    coupling_rows,
    coupling_columns,
    row_neighbours,
    column_neighbours,
    row_counts,
    column_counts,
):
    z = lax.axis_index("ia")
    here = lax.axis_index("ja")
    width = amplitudes.shape[-1]
    basis = pno_basis[0]
    depth = basis.shape[1]
    total_columns = coupling_columns.shape[0]
    block = jnp.concatenate([basis, amplitudes[0].astype(jnp.bfloat16)], axis=1)
    chunks = spread(block)
    mine_t = jnp.swapaxes(basis, 1, 2)
    own_t = jnp.concatenate([mine_t, swap(mine_t)], axis=0)
    slots = column_neighbours.shape[2]
    table = jnp.concatenate(
        [
            coupling_columns.T,
            column_neighbours[0].astype(jnp.float32),
            column_counts[0][:, None].astype(jnp.float32),
        ],
        axis=1,
    )
    table = jnp.pad(table, ((0, 0), (0, width - table.shape[1])))
    table = jnp.concatenate([table, swap(table)], axis=0)
    where = jnp.stack([z, here]).astype(jnp.int32)
    plan = make_plan(
        where,
        row_neighbours[0],
        table[:, total_columns : total_columns + slots].astype(jnp.int32),
        row_counts,
        table[:, total_columns + slots].astype(jnp.int32),
        coupling_rows,
        table[:, :total_columns],
    )
    domain_rows = lax.dynamic_slice_in_dim(domain_map, z, 1, 0)[0]
    domain_columns = lax.dynamic_slice_in_dim(domain_map, here * PAIRS, PAIRS, 1)
    other = here + 1 - 2 * (here % CORES)
    ours = lax.dynamic_slice_in_dim(domain_rows, here * PAIRS, PAIRS, 0)
    theirs = lax.dynamic_slice_in_dim(domain_rows, other * PAIRS, PAIRS, 0)
    doms = jnp.concatenate(
        [domain_rows, domain_columns.reshape(-1, depth), ours, theirs, ours, theirs], axis=0
    )
    gap = (
        pno_energy[0, :, :, None]
        + pno_energy[0, :, None, :]
        - row_energy[0]
        - column_energy[:, None, None]
    )
    exch = exchange_ints[0]
    current = amplitudes[0]
    zero = jnp.zeros((CHIP, width, width), jnp.float32)
    kept = {}
    acc = zero
    for n in COLUMN_ORDER:
        kept[n], acc = first_pass(n, plan, own_t, doms, acc, chunks[n])
    partner = swap(acc[PAIRS:])
    kept[ZCHUNK], acc = first_pass(ZCHUNK, plan, own_t, doms, acc, chunks[ZCHUNK])
    residual = exch + gap * current - (acc[:PAIRS] + partner)
    current = current - residual / (gap + level_shift)
    chunks = spread(current.astype(jnp.bfloat16))
    acc = zero
    for n in COLUMN_ORDER:
        acc = second_pass(n, plan, kept[n], acc, chunks[n])
    partner = swap(acc[PAIRS:])
    acc = second_pass(ZCHUNK, plan, kept[ZCHUNK], acc, chunks[ZCHUNK])
    current, energy = final(exch, gap, current, acc[:PAIRS], partner)
    return current[None], energy[None, :, 0, 0]


def solution(mesh):
    in_specs = (
        P("ia", "ja", None, None),
        P(),
        P("ia", "ja", None, None),
        P("ia", "ja", None, None),
        P("ia", "ja", None),
        P("ia"),
        P("ja"),
        P("ia", None),
        P(None, "ja"),
        P("ia", "ja", None),
        P("ia", "ja", None),
        P("ia", "ja"),
        P("ia", "ja"),
    )
    out_specs = (P("ia", "ja", None, None), P("ia", "ja"))
    return jax.shard_map(whole, mesh=mesh, in_specs=in_specs, out_specs=out_specs, check_vma=False)
```
